32 devices in a mesh: sec: 4 (over x, core), row: 8 (over z, y).
Axes of the slice: x: 2, y: 2, z: 4, core: 2. Of those that a mesh axis runs over, the one named last changes fastest.
Arguments:
- factor: float32 [4, 2048, 8192], P(None, 'row', 'sec'), may hold values from -0.0625 to 0.0625
- inverse_blocks: float32 [4, 2048, 2048], P('sec', 'row'), may hold values from -4 to 4, as said below
- right_side: float32 [4, 2048, 384], P('sec', 'row'), may hold values from -6 to 6
Outputs:
- solution: float32 [4, 2048, 384], P('sec', 'row')
The draws below stay inside these ranges and needn't reach their ends.
Inputs may be any that keep to these rules, and one draw needn't show every extreme that they name: `inverse_blocks`: each block is nonsingular; it stands for the inverse of the factor's diagonal block of that section.
All inputs are finite; a program needn't handle non-finite values.
Results may differ from the reference program's by a relative error of at most 0.0001.
Values sent between devices are 32-bit elements; how exact they have to be, the bound alone decides.
A program may use at most 64 MiB of HBM per device.

```python
import math
import jax
import jax.numpy as jnp
from jax import lax

BLOCK = 2048
ORDER = 8192
COLS = 384
N_SEC = 4


def draw_inverse_blocks(key, part):
    first = jax.random.fold_in(jax.random.fold_in(key, 17), 0)
    noise = jnp.clip(jax.random.normal(first, (N_SEC, BLOCK, BLOCK), jnp.float32), -6.0, 6.0)
    blocks = jnp.eye(BLOCK, dtype=jnp.float32)[None] + 0.5 * noise / math.sqrt(BLOCK)
    return blocks


def steps_of(stream_key, shape, cuts, low, top_value):
    factor_of = 1.0
    for dim, parts in cuts:
        draws = jax.random.uniform(jax.random.fold_in(jax.random.fold_in(stream_key, 6), dim), (parts,), jnp.float32, low / len(cuts), top_value / len(cuts))
        factor_of = factor_of * jnp.repeat(jnp.exp(draws), shape[dim] // parts).reshape((-1,) + (1,) * (len(shape) - 1 - dim))
    return factor_of


def centred(stream_key, shape, spread, most, shards=(), kind=jnp.bfloat16):
    level = steps_of(stream_key, shape, shards, -0.22, 0.18) if shards else 1.0
    drawn = jax.random.normal(stream_key, shape, jnp.float32) * spread * level
    return jnp.minimum(jnp.maximum(drawn, -most), most).astype(kind)


def setup_inputs(seed: int = 0) -> dict:
    key_of = jax.random.split(jax.random.key(seed), 4)
    factor = centred(key_of[0], (N_SEC, BLOCK, ORDER), ORDER ** -0.5, 0.0625, ((1, 8), (2, 4)), jnp.float32)
    inverse_blocks = draw_inverse_blocks(jax.random.fold_in(key_of[3], 71), 0)
    right_side = centred(key_of[2], (N_SEC, BLOCK, COLS), 1.0, 6.0, ((0, 4), (1, 8)), jnp.float32)
    return dict(factor=factor, inverse_blocks=inverse_blocks, right_side=right_side)


def reference(factor, inverse_blocks, right_side):
    carried = jnp.zeros(right_side.shape, jnp.float32)
    pieces = []
    for index in range(N_SEC):
        residual = right_side[index] - carried[index]
        result = jnp.dot(inverse_blocks[index], residual, precision=lax.Precision.HIGHEST)
        pieces.append(result)
        if index + 1 < N_SEC:
            block = factor[index + 1:, :, index * BLOCK:(index + 1) * BLOCK]
            update = jnp.einsum("ias,sw->iaw", block, result, precision=lax.Precision.HIGHEST)
            carried = carried.at[index + 1:].add(update)
    return jnp.stack(pieces)
```

```python
import functools

import jax
import jax.numpy as jnp
from jax import lax
from jax.experimental import pallas as pl
from jax.experimental.pallas import tpu as pltpu
from jax.sharding import PartitionSpec as P

MESH = pl.DeviceIdType.MESH
WIDTH = 128


def split(value):
    high = value.astype(jnp.bfloat16)
    low = (value - high.astype(jnp.float32)).astype(jnp.bfloat16)
    return high, low


def kernel(
    sections, lines, columns, micro,
    factor, inverse, rhs, out,
    staged, panels, residuals, solved, operand, product, arrived, leaving,
    load_sem, send_sem, recv_sem, part_send, part_recv,
):
    width = WIDTH
    rows = rhs.shape[0]
    group = lines * columns
    sec = lax.axis_index("sec")
    me = lax.axis_index("row")
    z, y = me // columns, me % columns
    z_steps = [s for d in range(1, lines) for s in ([d] if 2 * d == lines else [d, lines - d]) if 2 * d <= lines]
    z_peers = [lax.rem(z + s, lines) * columns + y for s in z_steps]
    y_peers = [z * columns + lax.rem(y + s, columns) for s in range(1, columns)]
    lines_of = [lax.rem(z + s, lines) for s in z_steps]

    def load(slot, source):
        return pltpu.make_async_copy(source, staged.at[slot], load_sem.at[slot])

    load(0, inverse).start()

    def start_load(i, carry):
        load(i, factor.at[i]).start()
        return carry

    lax.fori_loop(sec + 1, sections, start_load, 0)

    barrier = pltpu.get_barrier_semaphore()
    for peer in z_peers + y_peers:
        pl.semaphore_signal(barrier, inc=1, device_id=(sec, peer), device_id_type=MESH)
    for s in range(1, sections):
        pl.semaphore_signal(barrier, inc=1, device_id=(lax.rem(sec + s, sections), me), device_id_type=MESH)
    pl.semaphore_wait(barrier, len(z_peers) + len(y_peers) + sections - 1)

    def prepare(slot, carry):
        load(slot, factor.at[slot]).wait()
        step = 64 if rows % 64 == 0 else rows

        def part(j, carry):
            at = pl.multiple_of(j * step, step)
            high, low = split(staged[slot, pl.ds(at, step), :])
            panels[slot, pl.ds(at, step), :] = high
            panels[slot, pl.ds(pl.multiple_of(rows + at, step), step), :] = low
            return carry

        return lax.fori_loop(0, rows // step, part, carry)

    def place(source):
        return pl.ds(pl.multiple_of(source * rows, rows), rows)

    def copy_of(buffer, kind, c, source, number, peer):
        return pltpu.make_async_remote_copy(
            src_ref=buffer.at[c, place(source), :],
            dst_ref=buffer.at[c, place(source), :],
            send_sem=send_sem.at[kind, c, number],
            recv_sem=recv_sem.at[kind, c, source],
            device_id=(sec, peer),
            device_id_type=MESH,
        )

    def spread(buffer, kind, c):
        for number, peer in enumerate(z_peers + y_peers):
            copy_of(buffer, kind, c, me, number, peer).start()

    def digest(buffer, c, source):
        high, low = split(buffer[c, place(source), :])
        operand[place(source), pl.ds(0, width)] = high
        operand[place(source), pl.ds(width, width)] = low

    def relay(buffer, kind, c):
        number = len(z_peers) + len(y_peers)
        for peer in z_peers:
            copy_of(buffer, kind, c, peer, 0, me).wait_recv()
            for target in y_peers:
                copy_of(buffer, kind, c, peer, number, target).start()
                number += 1
            digest(buffer, c, peer)

    def finish(buffer, kind, c):
        digest(buffer, c, me)
        for s in range(1, columns):
            column = lax.rem(y + s, columns)
            for line in [z] + lines_of:
                source = line * columns + column
                copy_of(buffer, kind, c, source, 0, me).wait_recv()
                digest(buffer, c, source)

    def multiply(slot):
        product[...] = jnp.dot(panels[slot], operand[...], preferred_element_type=jnp.float32)
        upper = product[pl.ds(0, rows), pl.ds(0, width)] + product[pl.ds(0, rows), pl.ds(width, width)]
        lower = product[pl.ds(rows, rows), pl.ds(0, width)] + product[pl.ds(rows, rows), pl.ds(width, width)]
        return upper + lower

    def part_copy(source, target, c):
        return pltpu.make_async_remote_copy(
            src_ref=leaving.at[target, c],
            dst_ref=arrived.at[source, c],
            send_sem=part_send.at[target, c],
            recv_sem=part_recv.at[source, c],
            device_id=(target, me),
            device_id_type=MESH,
        )

    def begin(c):
        cols = pl.ds(pl.multiple_of(c * width, width), width)
        residuals[c, place(me), :] = rhs[:, cols]

        def subtract(k, carry):
            part_copy(k, sec, c).wait_recv()
            residuals[c, place(me), :] = residuals[c, place(me), :] - arrived[k, c]
            return carry

        lax.fori_loop(0, sec, subtract, 0)
        spread(residuals, 0, c)

    @pl.when(sec == 0)
    def _():
        begin(0)

    prepare(0, 0)
    lax.fori_loop(sec + 1, sections, prepare, 0)

    def advance(c, carry):
        @pl.when(sec > 0)
        def _():
            begin(c)

        relay(residuals, 0, c)

        @pl.when(jnp.logical_and(sec == 0, c + 1 < micro))
        def _():
            begin(c + 1)

        finish(residuals, 0, c)
        result = multiply(0)
        solved[c, place(me), :] = result
        out[:, pl.ds(pl.multiple_of(c * width, width), width)] = result

        @pl.when(sec + 1 < sections)
        def _():
            spread(solved, 1, c)
            relay(solved, 1, c)
            finish(solved, 1, c)

            def send(i, carry):
                leaving[i, c] = multiply(i)
                part_copy(sec, i, c).start()
                return carry

            lax.fori_loop(sec + 1, sections, send, 0)

        return carry

    lax.fori_loop(0, micro, advance, 0)

    def drain(c, carry):
        def sent(buffer, kind):
            for number in range(group - 1):
                copy_of(buffer, kind, c, me, number, me).wait_send()

        sent(residuals, 0)

        @pl.when(sec + 1 < sections)
        def _():
            sent(solved, 1)

            def wait_part(i, carry):
                part_copy(sec, i, c).wait_send()
                return carry

            lax.fori_loop(sec + 1, sections, wait_part, 0)

        return carry

    lax.fori_loop(0, micro, drain, 0)


def solution(mesh):
    sections, group = mesh.shape["sec"], mesh.shape["row"]
    columns = max(1, sections // 2)
    while group % columns:
        columns -= 1
    lines = group // columns

    def shards(factor, inverse_blocks, right_side):
        rows, depth = factor.shape[1], factor.shape[2]
        total = right_side.shape[2]
        micro = total // WIDTH
        bf16, f32 = jnp.bfloat16, jnp.float32
        result = pl.pallas_call(
            functools.partial(kernel, sections, lines, columns, micro),
            out_shape=jax.ShapeDtypeStruct((rows, total), f32),
            in_specs=[
                pl.BlockSpec(memory_space=pl.ANY),
                pl.BlockSpec(memory_space=pl.ANY),
                pl.BlockSpec(memory_space=pltpu.VMEM),
            ],
            out_specs=pl.BlockSpec(memory_space=pltpu.VMEM),
            scratch_shapes=[
                pltpu.VMEM((sections, rows, depth), f32),
                pltpu.VMEM((sections, 2 * rows, depth), bf16),
                pltpu.VMEM((micro, depth, WIDTH), f32),
                pltpu.VMEM((micro, depth, WIDTH), f32),
                pltpu.VMEM((depth, 2 * WIDTH), bf16),
                pltpu.VMEM((2 * rows, 2 * WIDTH), f32),
                pltpu.VMEM((sections, micro, rows, WIDTH), f32),
                pltpu.VMEM((sections, micro, rows, WIDTH), f32),
                pltpu.SemaphoreType.DMA((sections,)),
                pltpu.SemaphoreType.DMA((2, micro, group)),
                pltpu.SemaphoreType.DMA((2, micro, group)),
                pltpu.SemaphoreType.DMA((sections, micro)),
                pltpu.SemaphoreType.DMA((sections, micro)),
            ],
            compiler_params=pltpu.CompilerParams(
                collective_id=0, has_side_effects=True, vmem_limit_bytes=56 * 2**20
            ),
        )(factor, inverse_blocks[0], right_side[0])
        return result[None]

    return jax.shard_map(
        shards,
        mesh=mesh,
        in_specs=(P(None, "row", "sec"), P("sec", "row", None), P("sec", "row", None)),
        out_specs=P("sec", "row", None),
        check_vma=False,
    )
```

```python
import functools

import jax
import jax.numpy as jnp
from jax import lax
from jax.experimental import pallas as pl
from jax.experimental.pallas import tpu as pltpu
from jax.sharding import PartitionSpec as P

MESH = pl.DeviceIdType.MESH
WIDTH = 128
PIECES = 2


def split(value):
    high = value.astype(jnp.bfloat16)
    low = (value - high.astype(jnp.float32)).astype(jnp.bfloat16)
    return high, low


def kernel(
    sections, lines, columns, micro, pieces,
    factor, inverse, rhs, out,
    staged, panels, residuals, solved, operand, product, arrived, leaving,
    following, load_sem, send_sem, recv_sem, part_send, part_recv, hand_sem, rhs_sem,
):
    width = WIDTH
    rows = rhs.shape[0]
    group = lines * columns
    sec = lax.axis_index("sec")
    me = lax.axis_index("row")
    z, y = me // columns, me % columns
    z_steps = [s for d in range(1, lines) for s in ([d] if 2 * d == lines else [d, lines - d]) if 2 * d <= lines]
    z_peers = [lax.rem(z + s, lines) * columns + y for s in z_steps]
    y_peers = [z * columns + lax.rem(y + s, columns) for s in range(1, columns)]
    lines_of = [lax.rem(z + s, lines) for s in z_steps]

    def load(slot, source):
        return pltpu.make_async_copy(source, staged.at[slot], load_sem.at[slot])

    load(0, inverse).start()

    def start_load(i, carry):
        load(i, factor.at[i]).start()
        return carry

    lax.fori_loop(sec + 1, sections, start_load, 0)

    barrier = pltpu.get_barrier_semaphore()
    for peer in z_peers + y_peers:
        for s in (0, 1, sections - 1):
            pl.semaphore_signal(barrier, inc=1, device_id=(lax.rem(sec + s, sections), peer), device_id_type=MESH)
    for s in range(1, sections):
        pl.semaphore_signal(barrier, inc=1, device_id=(lax.rem(sec + s, sections), me), device_id_type=MESH)
    pl.semaphore_wait(barrier, 3 * (len(z_peers) + len(y_peers)) + sections - 1)

    def prepare(slot, carry):
        load(slot, factor.at[slot]).wait()
        step = 64 if rows % 64 == 0 else rows

        def part(j, carry):
            at = pl.multiple_of(j * step, step)
            high, low = split(staged[slot, pl.ds(at, step), :])
            panels[slot, pl.ds(at, step), :] = high
            panels[slot, pl.ds(pl.multiple_of(rows + at, step), step), :] = low
            return carry

        return lax.fori_loop(0, rows // step, part, carry)

    def place(source):
        return pl.ds(pl.multiple_of(source * rows, rows), rows)

    length = rows // pieces

    def part_of(source, piece):
        return pl.ds(pl.multiple_of(source * rows + piece * length, length), length)

    def copy_of(buffer, kind, c, source, piece, number, peer):
        return pltpu.make_async_remote_copy(
            src_ref=buffer.at[c, part_of(source, piece), :],
            dst_ref=buffer.at[c, part_of(source, piece), :],
            send_sem=send_sem.at[kind, c, number, piece],
            recv_sem=recv_sem.at[kind, c, source, piece],
            device_id=(sec, peer),
            device_id_type=MESH,
        )

    def spread(buffer, kind, c):
        for piece in range(pieces):
            for number, peer in enumerate(z_peers + y_peers):
                copy_of(buffer, kind, c, me, piece, number, peer).start()

    def digest(buffer, kind, c, source):
        high, low = split(buffer[c, place(source), :])
        operand[kind, place(source), pl.ds(0, width)] = high
        operand[kind, place(source), pl.ds(width, width)] = low

    def relay(buffer, kind, c):
        for piece in range(pieces):
            number = len(z_peers) + len(y_peers)
            for peer in z_peers:
                copy_of(buffer, kind, c, peer, piece, 0, me).wait_recv()
                for target in y_peers:
                    copy_of(buffer, kind, c, peer, piece, number, target).start()
                    number += 1
        for peer in z_peers:
            digest(buffer, kind, c, peer)

    def arrive(buffer, kind, c, source):
        for piece in range(pieces):
            copy_of(buffer, kind, c, source, piece, 0, me).wait_recv()
        digest(buffer, kind, c, source)

    def finish(buffer, kind, c):
        for s in range(1, columns):
            column = lax.rem(y + s, columns)
            for line in [z] + lines_of:
                arrive(buffer, kind, c, line * columns + column)

    def multiply(slot, kind):
        product[...] = jnp.dot(panels[slot], operand[kind], preferred_element_type=jnp.float32)
        upper = product[pl.ds(0, rows), pl.ds(0, width)] + product[pl.ds(0, rows), pl.ds(width, width)]
        lower = product[pl.ds(rows, rows), pl.ds(0, width)] + product[pl.ds(rows, rows), pl.ds(width, width)]
        return upper + lower

    def far_copy(source, target, c):
        return pltpu.make_async_remote_copy(
            src_ref=leaving.at[target, c],
            dst_ref=arrived.at[source, c],
            send_sem=part_send.at[target, c],
            recv_sem=part_recv.at[source, c],
            device_id=(target - 1, me),
            device_id_type=MESH,
        )

    def cols_of(c):
        return pl.ds(pl.multiple_of(c * width, width), width)

    def begin(c):
        residuals[c, place(me), :] = rhs[:, cols_of(c)]
        spread(residuals, 0, c)
        digest(residuals, 0, c, me)

    def hand_copy(c, piece, number, peer):
        return pltpu.make_async_remote_copy(
            src_ref=leaving.at[0, c, pl.ds(piece * length, length), :],
            dst_ref=residuals.at[c, part_of(me, piece), :],
            send_sem=hand_sem.at[c, number, piece],
            recv_sem=recv_sem.at[0, c, me, piece],
            device_id=(sec + 1, peer),
            device_id_type=MESH,
        )

    def hand_on(c):
        leaving[0, c] = following[:, cols_of(c)] - multiply(sec + 1, 1)

        def subtract(k, carry):
            far_copy(k, sec + 1, c).wait_recv()
            leaving[0, c] = leaving[0, c] - arrived[k, c]
            return carry

        lax.fori_loop(0, sec, subtract, 0)
        for piece in range(pieces):
            for number, peer in enumerate(z_peers + y_peers + [me]):
                hand_copy(c, piece, number, peer).start()

    def rhs_copy():
        return pltpu.make_async_remote_copy(
            src_ref=rhs, dst_ref=following, send_sem=rhs_sem.at[0], recv_sem=rhs_sem.at[1],
            device_id=(sec - 1, me), device_id_type=MESH,
        )

    last = sec + 1 == sections

    @pl.when(sec == 0)
    def _():
        begin(0)

    @pl.when(sec > 0)
    def _():
        rhs_copy().start()

    prepare(0, 0)

    @pl.when(sec > 0)
    def _():
        lax.fori_loop(sec + 1, sections, prepare, 0)

    relay(residuals, 0, 0)

    def send(i, c):
        leaving[i, c] = multiply(i, 1)
        far_copy(sec, i, c).start()
        return c

    def advance(c, carry):
        more = c + 1 < micro

        @pl.when(sec > 0)
        def _():
            arrive(residuals, 0, c, me)

        finish(residuals, 0, c)
        result = multiply(0, 0)
        solved[c, place(me), :] = result

        @pl.when(jnp.logical_not(last))
        def _():
            spread(solved, 1, c)
            digest(solved, 1, c, me)

        out[:, cols_of(c)] = result

        @pl.when(jnp.logical_and(sec == 0, more))
        def _():
            begin(c + 1)

        @pl.when(jnp.logical_and(sec == 0, c == 0))
        def _():
            lax.fori_loop(1, sections, prepare, 0)

        @pl.when(jnp.logical_not(last))
        def _():
            @pl.when(c == 0)
            def _():
                pltpu.make_async_remote_copy(
                    src_ref=rhs, dst_ref=following, send_sem=rhs_sem.at[0], recv_sem=rhs_sem.at[1],
                    device_id=(sec, me), device_id_type=MESH,
                ).wait_recv()

            relay(solved, 1, c)
            @pl.when(more)
            def _():
                relay(residuals, 0, c + 1)

            finish(solved, 1, c)
            hand_on(c)

        @pl.when(jnp.logical_and(last, more))
        def _():
            relay(residuals, 0, c + 1)

        lax.fori_loop(sec + 2, sections, send, c)
        return carry

    lax.fori_loop(0, micro, advance, 0)

    def drain(c, carry):
        for piece in range(pieces):
            for number in range(group - 1):
                own = len(z_peers) + len(y_peers)

                def sent():
                    copy_of(residuals, 0, c, me, piece, number, me).wait_send()

                if number >= own:
                    sent()
                else:
                    pl.when(sec == 0)(sent)

            @pl.when(jnp.logical_not(last))
            def _():
                for number in range(group - 1):
                    copy_of(solved, 1, c, me, piece, number, me).wait_send()
                for number in range(len(z_peers) + len(y_peers) + 1):
                    hand_copy(c, piece, number, me).wait_send()

        def wait_far(i, carry):
            far_copy(sec, i, c).wait_send()
            return carry

        lax.fori_loop(sec + 2, sections, wait_far, 0)
        return carry

    lax.fori_loop(0, micro, drain, 0)

    @pl.when(sec > 0)
    def _():
        rhs_copy().wait_send()


def solution(mesh):
    sections, group = mesh.shape["sec"], mesh.shape["row"]
    columns = max(1, sections // 2)
    while group % columns:
        columns -= 1
    lines = group // columns

    def shards(factor, inverse_blocks, right_side):
        rows, depth = factor.shape[1], factor.shape[2]
        total = right_side.shape[2]
        micro = total // WIDTH
        pieces = PIECES if rows % (8 * PIECES) == 0 else 1
        bf16, f32 = jnp.bfloat16, jnp.float32
        result = pl.pallas_call(
            functools.partial(kernel, sections, lines, columns, micro, pieces),
            out_shape=jax.ShapeDtypeStruct((rows, total), f32),
            in_specs=[
                pl.BlockSpec(memory_space=pl.ANY),
                pl.BlockSpec(memory_space=pl.ANY),
                pl.BlockSpec(memory_space=pltpu.VMEM),
            ],
            out_specs=pl.BlockSpec(memory_space=pltpu.VMEM),
            scratch_shapes=[
                pltpu.VMEM((sections, rows, depth), f32),
                pltpu.VMEM((sections, 2 * rows, depth), bf16),
                pltpu.VMEM((micro, depth, WIDTH), f32),
                pltpu.VMEM((micro, depth, WIDTH), f32),
                pltpu.VMEM((2, depth, 2 * WIDTH), bf16),
                pltpu.VMEM((2 * rows, 2 * WIDTH), f32),
                pltpu.VMEM((sections, micro, rows, WIDTH), f32),
                pltpu.VMEM((sections, micro, rows, WIDTH), f32),
                pltpu.VMEM((rows, total), f32),
                pltpu.SemaphoreType.DMA((sections,)),
                pltpu.SemaphoreType.DMA((2, micro, group, pieces)),
                pltpu.SemaphoreType.DMA((2, micro, group, pieces)),
                pltpu.SemaphoreType.DMA((sections, micro)),
                pltpu.SemaphoreType.DMA((sections, micro)),
                pltpu.SemaphoreType.DMA((micro, lines + columns - 1, pieces)),
                pltpu.SemaphoreType.DMA((2,)),
            ],
            compiler_params=pltpu.CompilerParams(
                collective_id=0, has_side_effects=True, vmem_limit_bytes=56 * 2**20
            ),
        )(factor, inverse_blocks[0], right_side[0])
        return result[None]

    return jax.shard_map(
        shards,
        mesh=mesh,
        in_specs=(P(None, "row", "sec"), P("sec", "row", None), P("sec", "row", None)),
        out_specs=P("sec", "row", None),
        check_vma=False,
    )
```

```python
import functools

import jax
import jax.numpy as jnp
from jax import lax
from jax.experimental import pallas as pl
from jax.experimental.pallas import tpu as pltpu
from jax.sharding import PartitionSpec as P

MESH = pl.DeviceIdType.MESH
WIDTH = 128
PIECES = 2


def split(value):
    high = value.astype(jnp.bfloat16)
    low = (value - high.astype(jnp.float32)).astype(jnp.bfloat16)
    return high, low


def kernel(
    sections, lines, columns, micro, pieces,
    factor, inverse, rhs, out,
    staged, panels, residuals, solved, operand, product, arrived, leaving,
    following, load_sem, send_sem, recv_sem, part_send, part_recv, hand_sem, rhs_sem,
):
    width = WIDTH
    rows = rhs.shape[0]
    group = lines * columns
    sec = lax.axis_index("sec")
    me = lax.axis_index("row")
    z, y = me // columns, me % columns
    z_steps = [s for d in range(1, lines) for s in ([d] if 2 * d == lines else [d, lines - d]) if 2 * d <= lines]
    z_peers = [lax.rem(z + s, lines) * columns + y for s in z_steps]
    y_peers = [z * columns + lax.rem(y + s, columns) for s in range(1, columns)]
    lines_of = [lax.rem(z + s, lines) for s in z_steps]
    half = lines // 2 if lines % 2 == 0 else lines
    side = z // half
    mates = [(side * half + lax.rem(z + s, half)) * columns + y for s in range(1, half)]
    gate = half - 1 + side
    is_gate = z == gate
    far_lines = [half - side + j * (1 - 2 * side) for j in range(half)] if half < lines else []
    far = [line * columns + y for line in far_lines]
    targets = mates + far[:1] + y_peers
    relayed = (lines - 1) * (columns - 1)

    def load(slot, source):
        return pltpu.make_async_copy(source, staged.at[slot], load_sem.at[slot])

    load(0, inverse).start()

    def start_load(i, carry):
        load(i, factor.at[i]).start()
        return carry

    lax.fori_loop(sec + 1, sections, start_load, 0)

    barrier = pltpu.get_barrier_semaphore()
    for peer in z_peers + y_peers:
        for s in (0, 1, sections - 1):
            pl.semaphore_signal(barrier, inc=1, device_id=(lax.rem(sec + s, sections), peer), device_id_type=MESH)
    for s in range(1, sections):
        pl.semaphore_signal(barrier, inc=1, device_id=(lax.rem(sec + s, sections), me), device_id_type=MESH)
    pl.semaphore_wait(barrier, 3 * (len(z_peers) + len(y_peers)) + sections - 1)

    def prepare(slot, carry):
        load(slot, factor.at[slot]).wait()
        step = 64 if rows % 64 == 0 else rows

        def part(j, carry):
            at = pl.multiple_of(j * step, step)
            high, low = split(staged[slot, pl.ds(at, step), :])
            panels[slot, pl.ds(at, step), :] = high
            panels[slot, pl.ds(pl.multiple_of(rows + at, step), step), :] = low
            return carry

        return lax.fori_loop(0, rows // step, part, carry)

    def place(source):
        return pl.ds(pl.multiple_of(source * rows, rows), rows)

    length = rows // pieces

    def part_of(source, piece):
        return pl.ds(pl.multiple_of(source * rows + piece * length, length), length)

    def copy_of(buffer, kind, c, source, piece, number, peer):
        return pltpu.make_async_remote_copy(
            src_ref=buffer.at[c, part_of(source, piece), :],
            dst_ref=buffer.at[c, part_of(source, piece), :],
            send_sem=send_sem.at[kind, c, number, piece],
            recv_sem=recv_sem.at[kind, c, source, piece],
            device_id=(sec, peer),
            device_id_type=MESH,
        )

    def spread(buffer, kind, c):
        for piece in range(pieces):
            for number, peer in enumerate(targets):
                copy_of(buffer, kind, c, me, piece, number, peer).start()

    def digest(buffer, kind, c, source):
        high, low = split(buffer[c, place(source), :])
        operand[kind, place(source), pl.ds(0, width)] = high
        operand[kind, place(source), pl.ds(width, width)] = low

    def relay(buffer, kind, c):
        for piece in range(pieces):
            number = len(targets)
            inner = number + relayed
            for peer in mates + far:
                copy_of(buffer, kind, c, peer, piece, 0, me).wait_recv()
                if any(peer is source for source in far) and mates:
                    def pass_on(peer=peer, inner=inner):
                        for step, mate in enumerate(mates):
                            copy_of(buffer, kind, c, peer, piece, inner + step, mate).start()

                    pl.when(is_gate)(pass_on)
                    inner += len(mates)
                for target in y_peers:
                    copy_of(buffer, kind, c, peer, piece, number, target).start()
                    number += 1
        for peer in mates + far:
            digest(buffer, kind, c, peer)

    def arrive(buffer, kind, c, source):
        for piece in range(pieces):
            copy_of(buffer, kind, c, source, piece, 0, me).wait_recv()
        digest(buffer, kind, c, source)

    def finish(buffer, kind, c):
        for s in range(1, columns):
            column = lax.rem(y + s, columns)
            for line in [z] + lines_of:
                arrive(buffer, kind, c, line * columns + column)

    def multiply(slot, kind):
        product[...] = jnp.dot(panels[slot], operand[kind], preferred_element_type=jnp.float32)
        upper = product[pl.ds(0, rows), pl.ds(0, width)] + product[pl.ds(0, rows), pl.ds(width, width)]
        lower = product[pl.ds(rows, rows), pl.ds(0, width)] + product[pl.ds(rows, rows), pl.ds(width, width)]
        return upper + lower

    def far_copy(source, target, c):
        return pltpu.make_async_remote_copy(
            src_ref=leaving.at[target, c],
            dst_ref=arrived.at[source, c],
            send_sem=part_send.at[target, c],
            recv_sem=part_recv.at[source, c],
            device_id=(target - 1, me),
            device_id_type=MESH,
        )

    def cols_of(c):
        return pl.ds(pl.multiple_of(c * width, width), width)

    def begin(c):
        residuals[c, place(me), :] = rhs[:, cols_of(c)]
        spread(residuals, 0, c)
        digest(residuals, 0, c, me)

    def hand_copy(c, piece, number, peer):
        return pltpu.make_async_remote_copy(
            src_ref=leaving.at[0, c, pl.ds(piece * length, length), :],
            dst_ref=residuals.at[c, part_of(me, piece), :],
            send_sem=hand_sem.at[c, number, piece],
            recv_sem=recv_sem.at[0, c, me, piece],
            device_id=(sec + 1, peer),
            device_id_type=MESH,
        )

    def hand_on(c):
        leaving[0, c] = following[:, cols_of(c)] - multiply(sec + 1, 1)

        def subtract(k, carry):
            far_copy(k, sec + 1, c).wait_recv()
            leaving[0, c] = leaving[0, c] - arrived[k, c]
            return carry

        lax.fori_loop(0, sec, subtract, 0)
        for piece in range(pieces):
            for number, peer in enumerate(targets + [me]):
                hand_copy(c, piece, number, peer).start()

    def rhs_copy():
        return pltpu.make_async_remote_copy(
            src_ref=rhs, dst_ref=following, send_sem=rhs_sem.at[0], recv_sem=rhs_sem.at[1],
            device_id=(sec - 1, me), device_id_type=MESH,
        )

    last = sec + 1 == sections

    @pl.when(sec == 0)
    def _():
        begin(0)

    @pl.when(sec > 0)
    def _():
        rhs_copy().start()

    prepare(0, 0)

    @pl.when(sec > 0)
    def _():
        lax.fori_loop(sec + 1, sections, prepare, 0)

    relay(residuals, 0, 0)

    def send(i, c):
        leaving[i, c] = multiply(i, 1)
        far_copy(sec, i, c).start()
        return c

    def advance(c, carry):
        more = c + 1 < micro

        @pl.when(sec > 0)
        def _():
            arrive(residuals, 0, c, me)

        finish(residuals, 0, c)
        result = multiply(0, 0)
        solved[c, place(me), :] = result

        @pl.when(jnp.logical_not(last))
        def _():
            spread(solved, 1, c)
            digest(solved, 1, c, me)

        out[:, cols_of(c)] = result

        @pl.when(jnp.logical_and(sec == 0, more))
        def _():
            begin(c + 1)

        @pl.when(jnp.logical_and(sec == 0, c == 0))
        def _():
            lax.fori_loop(1, sections, prepare, 0)

        @pl.when(jnp.logical_not(last))
        def _():
            @pl.when(c == 0)
            def _():
                pltpu.make_async_remote_copy(
                    src_ref=rhs, dst_ref=following, send_sem=rhs_sem.at[0], recv_sem=rhs_sem.at[1],
                    device_id=(sec, me), device_id_type=MESH,
                ).wait_recv()

            relay(solved, 1, c)
            @pl.when(more)
            def _():
                relay(residuals, 0, c + 1)

            finish(solved, 1, c)
            hand_on(c)

        @pl.when(jnp.logical_and(last, more))
        def _():
            relay(residuals, 0, c + 1)

        lax.fori_loop(sec + 2, sections, send, c)
        return carry

    lax.fori_loop(0, micro, advance, 0)

    def drain(c, carry):
        def sent(buffer, kind, numbers):
            for piece in range(pieces):
                for number in numbers:
                    copy_of(buffer, kind, c, me, piece, number, me).wait_send()

        own = range(len(targets))
        across = range(len(targets), len(targets) + relayed)
        inside = range(len(targets) + relayed, len(targets) + relayed + len(far) * len(mates))
        sent(residuals, 0, across)

        @pl.when(sec == 0)
        def _():
            sent(residuals, 0, own)

        @pl.when(is_gate)
        def _():
            sent(residuals, 0, inside)

        @pl.when(jnp.logical_not(last))
        def _():
            sent(solved, 1, own)
            sent(solved, 1, across)

            @pl.when(is_gate)
            def _():
                sent(solved, 1, inside)

            for piece in range(pieces):
                for number in range(len(targets) + 1):
                    hand_copy(c, piece, number, me).wait_send()

        def wait_far(i, carry):
            far_copy(sec, i, c).wait_send()
            return carry

        lax.fori_loop(sec + 2, sections, wait_far, 0)
        return carry

    lax.fori_loop(0, micro, drain, 0)

    @pl.when(sec > 0)
    def _():
        rhs_copy().wait_send()


def solution(mesh):
    sections, group = mesh.shape["sec"], mesh.shape["row"]
    columns = max(1, sections // 2)
    while group % columns:
        columns -= 1
    lines = group // columns

    def shards(factor, inverse_blocks, right_side):
        rows, depth = factor.shape[1], factor.shape[2]
        total = right_side.shape[2]
        micro = total // WIDTH
        pieces = PIECES if rows % (8 * PIECES) == 0 else 1
        half = lines // 2 if lines % 2 == 0 else lines
        numbers = half + columns - 1 + (lines - 1) * (columns - 1) + half * (half - 1)
        bf16, f32 = jnp.bfloat16, jnp.float32
        result = pl.pallas_call(
            functools.partial(kernel, sections, lines, columns, micro, pieces),
            out_shape=jax.ShapeDtypeStruct((rows, total), f32),
            in_specs=[
                pl.BlockSpec(memory_space=pl.ANY),
                pl.BlockSpec(memory_space=pl.ANY),
                pl.BlockSpec(memory_space=pltpu.VMEM),
            ],
            out_specs=pl.BlockSpec(memory_space=pltpu.VMEM),
            scratch_shapes=[
                pltpu.VMEM((sections, rows, depth), f32),
                pltpu.VMEM((sections, 2 * rows, depth), bf16),
                pltpu.VMEM((micro, depth, WIDTH), f32),
                pltpu.VMEM((micro, depth, WIDTH), f32),
                pltpu.VMEM((2, depth, 2 * WIDTH), bf16),
                pltpu.VMEM((2 * rows, 2 * WIDTH), f32),
                pltpu.VMEM((sections, micro, rows, WIDTH), f32),
                pltpu.VMEM((sections, micro, rows, WIDTH), f32),
                pltpu.VMEM((rows, total), f32),
                pltpu.SemaphoreType.DMA((sections,)),
                pltpu.SemaphoreType.DMA((2, micro, numbers, pieces)),
                pltpu.SemaphoreType.DMA((2, micro, group, pieces)),
                pltpu.SemaphoreType.DMA((sections, micro)),
                pltpu.SemaphoreType.DMA((sections, micro)),
                pltpu.SemaphoreType.DMA((micro, lines + columns - 1, pieces)),
                pltpu.SemaphoreType.DMA((2,)),
            ],
            compiler_params=pltpu.CompilerParams(
                collective_id=0, has_side_effects=True, vmem_limit_bytes=56 * 2**20
            ),
        )(factor, inverse_blocks[0], right_side[0])
        return result[None]

    return jax.shard_map(
        shards,
        mesh=mesh,
        in_specs=(P(None, "row", "sec"), P("sec", "row", None), P("sec", "row", None)),
        out_specs=P("sec", "row", None),
        check_vma=False,
    )
```
